32 devices in a mesh: gx: 16 (over z, y, core), gy: 2 (over x).
Axes of the slice: x: 2, y: 2, z: 4, core: 2. Of those that a mesh axis runs over, the one named last changes fastest.
Arguments:
- curves: float32 [16, 2, 4, 8, 128], P('gx', 'gy'), as said below
- curve_counts: int32 [16, 2], P('gx', 'gy'), may hold values from 1 to 8, as said below
- near_counts: int32 [16, 2], P('gx', 'gy'), may hold values from 204 to 1024, as said below
- near_lists: int32 [16, 2, 2, 1024], P('gx', 'gy'), may hold values from 0 to 2303, as said below
Outputs:
- velocity: float32 [16, 2, 2, 8, 128], P('gx', 'gy')
The draws below stay inside these ranges and needn't reach their ends.
Inputs may be any that keep to these rules, and one draw needn't show every extreme that they name: `curves`: components 0 and 1 are tile-local positions; each curve is closed and star-shaped about a centre that lies inside the tile's unit square, and all its nodes lie within 0.1 of that square; nodes at equally spaced parameter values, counterclockwise; components 2 and 3 are force densities. `curve_counts`: slots below the count hold curves, the others padding; some tile is full. `near_counts`: entries below the count are valid, the rest padding; some tile's list is full. `near_lists`: row 0: target node curve * 128 + node of the own tile. Row 1: source panel (slot * 8 + curve) * 32 + panel, slot 3 (a + 1) + (b + 1) for the tile at offset (a, b).
All inputs are finite; a program needn't handle non-finite values.
Results may differ from the reference program's by a relative error of at most 0.0003.
Values sent between devices are 32-bit elements; how exact they have to be, the bound alone decides.
A program may use at most 64 MiB of HBM per device.

```python
import math
import jax
import jax.numpy as jnp
import numpy as np
from jax import lax

NODES = 128
FINE = 512
PANEL = 16
REFINE = 4
CURVES = 8
NTX = 16
NTY = 2
NEAR = 1024


def draw_curves(key, part):
    subkeys = jax.random.split(key, 14)
    grid_shape = (NTX, NTY, CURVES)
    radius = jnp.exp(jax.random.uniform(subkeys[2], grid_shape, minval=math.log(0.03), maxval=math.log(0.3)))
    second_amp = jax.random.uniform(subkeys[3], grid_shape, minval=0.0, maxval=0.2)
    third_amp = jax.random.uniform(subkeys[4], grid_shape, minval=0.0, maxval=0.15)
    ripple_amp = jax.random.uniform(subkeys[9], grid_shape, minval=0.0, maxval=0.15)
    second_phase = jax.random.uniform(subkeys[5], grid_shape, minval=-math.pi, maxval=math.pi)
    third_phase = jax.random.uniform(subkeys[6], grid_shape, minval=-math.pi, maxval=math.pi)
    ripple_phase = jax.random.uniform(subkeys[10], grid_shape, minval=-math.pi, maxval=math.pi)
    ripple_mode = jax.random.randint(subkeys[11], grid_shape, 20, 29).astype(jnp.float32)
    reach = radius * (1.0 + second_amp + third_amp + ripple_amp)
    lowest = jnp.maximum(0.0, reach - 0.1)
    highest = jnp.minimum(1.0, 1.1 - reach)
    centre_x = lowest + (highest - lowest) * jax.random.uniform(subkeys[0], grid_shape, minval=0.0, maxval=1.0)
    centre_y = lowest + (highest - lowest) * jax.random.uniform(subkeys[1], grid_shape, minval=0.0, maxval=1.0)
    angles = 2.0 * math.pi * jnp.arange(NODES).astype(jnp.float32) / NODES
    shape_radius = radius[..., None] * (1.0 + second_amp[..., None] * jnp.cos(2.0 * angles + second_phase[..., None]) + third_amp[..., None] * jnp.cos(3.0 * angles + third_phase[..., None]) + ripple_amp[..., None] * jnp.cos(ripple_mode[..., None] * angles + ripple_phase[..., None]))
    pos_x = centre_x[..., None] + shape_radius * jnp.cos(angles)
    pos_y = centre_y[..., None] + shape_radius * jnp.sin(angles)
    mode_numbers = jnp.arange(5).astype(jnp.float32)
    mode_angles = mode_numbers[:, None] * angles[None, :]
    coeff_shape = (NTX, NTY, 2, CURVES, 5, 1)
    jitter = 20.0 * jax.random.normal(subkeys[7], (NTX, NTY, 2, CURVES, NODES))
    cos_coeff = jax.random.normal(subkeys[12], coeff_shape)
    sin_coeff = jax.random.normal(subkeys[13], coeff_shape)
    smooth = jnp.sum(cos_coeff * jnp.cos(mode_angles) + sin_coeff * jnp.sin(mode_angles), axis=-2)
    size_scale = (0.05 / radius)[:, :, None, :, None]
    forcing = size_scale * (jitter - jnp.roll(jitter, -1, axis=-1) + 0.6 * smooth)
    return jnp.concatenate([pos_x[:, :, None], pos_y[:, :, None], forcing], axis=2).astype(jnp.float32)


def skewed_counts(key, capacity, lowest):
    subkeys = jax.random.split(key, 3)
    first_draw = jax.random.randint(subkeys[0], (NTX, NTY), 0, capacity + 1)
    second_draw = jax.random.randint(subkeys[1], (NTX, NTY), 0, capacity + 1)
    counts = jnp.minimum(capacity, lowest + first_draw * second_draw // capacity)
    chosen = jax.random.randint(subkeys[2], (), 0, NTX * NTY)
    tile_index = jnp.arange(NTX * NTY).reshape(NTX, NTY)
    return jnp.where(tile_index == chosen, capacity, counts).astype(jnp.int32)


def draw_curve_counts(key, part):
    return skewed_counts(jax.random.fold_in(key, 11), CURVES, 1)


def draw_near_counts(key, part):
    return skewed_counts(jax.random.fold_in(key, 23), NEAR, NEAR // 5)


def draw_near_lists(key, part):
    subkeys = jax.random.split(jax.random.fold_in(key, 37), 4)
    panels = FINE // PANEL
    list_shape = (NTX, NTY, NEAR)
    target = jax.random.randint(subkeys[0], list_shape, 0, CURVES * NODES)
    same_curve = jax.random.randint(subkeys[1], list_shape, 0, 4) < 3
    node_index = target % NODES
    target_curve = target // NODES
    panel_step = jax.random.randint(subkeys[2], list_shape, -1, 2)
    near_panel = (node_index * (FINE // NODES) // PANEL + panel_step + panels) % panels
    own_source = (4 * CURVES + target_curve) * panels + near_panel
    other_source = jax.random.randint(subkeys[3], list_shape, 0, 9 * CURVES * panels)
    source = jnp.where(same_curve, own_source, other_source)
    return jnp.stack([target, source], axis=2).astype(jnp.int32)


def setup_inputs(seed: int = 0) -> dict:
    arg_keys = jax.random.split(jax.random.key(seed), 5)
    return {
        "curves": draw_curves(jax.random.fold_in(arg_keys[4], 71), 0),
        "curve_counts": draw_curve_counts(jax.random.fold_in(arg_keys[4], 71), 0),
        "near_counts": draw_near_counts(jax.random.fold_in(arg_keys[4], 71), 0),
        "near_lists": draw_near_lists(jax.random.fold_in(arg_keys[4], 71), 0),
    }


SOFT_SQ = 1e-08
HIGH = lax.Precision.HIGHEST

def spectral_tables(coarse_count, fine_count):
    coarse_index = np.arange(coarse_count)[:, None, None]
    fine_index = np.arange(fine_count)[None, :, None]
    modes = np.arange(1, coarse_count // 2)[None, None, :]
    nyquist = coarse_count // 2
    offset = 2.0 * np.pi * (fine_index / fine_count - coarse_index / coarse_count)
    upsample_table = (1.0 + 2.0 * np.sum(np.cos(modes * offset), axis=-1) + np.cos(nyquist * offset[..., 0])) / coarse_count
    derive_table = (-2.0 * np.sum(modes * np.sin(modes * offset), axis=-1) - nyquist * np.sin(nyquist * offset[..., 0])) / coarse_count
    return (jnp.asarray(upsample_table, dtype=jnp.float32), jnp.asarray(derive_table, dtype=jnp.float32))

def lagrange_table(panel_nodes, refine_factor):
    weights_table = np.zeros((panel_nodes + 3, panel_nodes * refine_factor))
    for column in range(panel_nodes * refine_factor):
        fraction = column % refine_factor / refine_factor
        start_node = column // refine_factor
        weights_table[start_node, column] = -fraction * (fraction - 1.0) * (fraction - 2.0) / 6.0
        weights_table[start_node + 1, column] = (fraction + 1.0) * (fraction - 1.0) * (fraction - 2.0) / 2.0
        weights_table[start_node + 2, column] = -(fraction + 1.0) * fraction * (fraction - 2.0) / 2.0
        weights_table[start_node + 3, column] = (fraction + 1.0) * fraction * (fraction - 1.0) / 6.0
    return jnp.asarray(weights_table, dtype=jnp.float32)

def stokeslet(sep_x, sep_y, push_x, push_y):
    dist_sq = sep_x * sep_x + sep_y * sep_y + SOFT_SQ
    half_log = 0.5 * jnp.log(dist_sq)
    projected = (sep_x * push_x + sep_y * push_y) / dist_sq
    return (projected * sep_x - half_log * push_x, projected * sep_y - half_log * push_y)

def upsample(block, upsample_table, derive_table):
    points = jnp.matmul(block[..., 0:2, :, :], upsample_table, precision=HIGH)
    tangent = jnp.matmul(block[..., 0:2, :, :], derive_table, precision=HIGH)
    tangent_x = tangent[..., 0, :, :]
    tangent_y = tangent[..., 1, :, :]
    speed = jnp.sqrt(tangent_x * tangent_x + tangent_y * tangent_y) * (2.0 * math.pi / FINE)
    pushes = jnp.matmul(block[..., 2:4, :, :], upsample_table, precision=HIGH) * speed[..., None, :, :]
    return jnp.concatenate([points, pushes], axis=-3)

def place_tiles(extended):
    shifts = (jnp.arange(3, dtype=jnp.int32) - 1).astype(jnp.float32)
    pos_x = extended[:, :, 0] + shifts[:, None, None, None]
    pos_y = extended[:, :, 1] + shifts[None, :, None, None]
    placed = jnp.stack([pos_x, pos_y, extended[:, :, 2], extended[:, :, 3]], axis=2)
    return placed.reshape(9, 4, -1)

def near_field(targ_x, targ_y, stacked):

    def visit(carry, slot_data):
        vel_x, vel_y = stokeslet(targ_x[:, None] - slot_data[0][None, :], targ_y[:, None] - slot_data[1][None, :], slot_data[2][None, :], slot_data[3][None, :])
        return ((carry[0] + lax.optimization_barrier(jnp.sum(vel_x, axis=1)), carry[1] + lax.optimization_barrier(jnp.sum(vel_y, axis=1))), None)
    zeros = jnp.zeros(targ_x.shape, jnp.float32)
    totals, unused = lax.scan(visit, (zeros, zeros), stacked)
    return totals

def corrections(targ_x, targ_y, stacked, near_count, near_list, refine_table):
    panels = FINE // PANEL
    flat_sources = jnp.transpose(stacked, (1, 0, 2)).reshape(4, -1)
    target = near_list[0]
    source = near_list[1]
    slot_curve = source // panels
    panel_index = source % panels
    window = (jnp.arange(PANEL + 3, dtype=jnp.int32) - 1).astype(jnp.int32)
    node_index = (panel_index[None, :] * PANEL + window[:, None]) % FINE
    flat_index = (slot_curve[None, :] * FINE + node_index).astype(jnp.int32)
    gathered = flat_sources[:, flat_index]
    refined = jnp.einsum('ic,kin->kcn', refine_table, gathered, precision=HIGH)
    point_x = targ_x[target]
    point_y = targ_y[target]
    fine_x, fine_y = stokeslet(point_x[None, :] - refined[0], point_y[None, :] - refined[1], refined[2], refined[3])
    inner = gathered[:, 1:PANEL + 1]
    coarse_x, coarse_y = stokeslet(point_x[None, :] - inner[0], point_y[None, :] - inner[1], inner[2], inner[3])
    in_list = (jnp.arange(near_list.shape[1], dtype=jnp.int32) < near_count).astype(jnp.float32)
    corr_x = (1.0 / REFINE * lax.optimization_barrier(jnp.sum(fine_x, axis=0)) - lax.optimization_barrier(jnp.sum(coarse_x, axis=0))) * in_list
    corr_y = (1.0 / REFINE * lax.optimization_barrier(jnp.sum(fine_y, axis=0)) - lax.optimization_barrier(jnp.sum(coarse_y, axis=0))) * in_list
    return (target, corr_x, corr_y)

def tile_velocity(extended, own_tile, living, near_count, near_list, refine_table):
    stacked = place_tiles(extended)
    targ_x = own_tile[0].reshape(-1)
    targ_y = own_tile[1].reshape(-1)
    vel_x, vel_y = near_field(targ_x, targ_y, stacked)
    target, corr_x, corr_y = corrections(targ_x, targ_y, stacked, near_count, near_list, refine_table)
    vel_x = vel_x.at[target].add(corr_x)
    vel_y = vel_y.at[target].add(corr_y)
    live_nodes = (living[:, None] * jnp.ones((1, NODES), jnp.float32)).reshape(-1)
    return jnp.stack([vel_x * live_nodes, vel_y * live_nodes]).reshape(2, CURVES, NODES)

def reference(curves, curve_counts, near_counts, near_lists):
    upsample_table, derive_table = spectral_tables(NODES, FINE)
    refine_table = lagrange_table(PANEL, REFINE)
    living = (jnp.arange(CURVES, dtype=jnp.int32)[None, None, :] < curve_counts[:, :, None]).astype(jnp.float32)
    masked = jnp.concatenate([curves[:, :, 0:2], curves[:, :, 2:4] * living[:, :, None, :, None]], axis=2)
    fine_nodes = upsample(masked, upsample_table, derive_table)

    def one_tile(tile_index):
        tile_row = tile_index // NTY
        tile_col = tile_index % NTY
        near_rows = ((tile_row + jnp.arange(3, dtype=jnp.int32) - 1) % NTX).astype(jnp.int32)
        near_cols = ((tile_col + jnp.arange(3, dtype=jnp.int32) - 1) % NTY).astype(jnp.int32)
        extended = jnp.take(jnp.take(fine_nodes, near_rows, axis=0), near_cols, axis=1)
        return tile_velocity(extended, curves[tile_row, tile_col], living[tile_row, tile_col], near_counts[tile_row, tile_col], near_lists[tile_row, tile_col], refine_table)
    velocity = lax.map(one_tile, jnp.arange(NTX * NTY, dtype=jnp.int32))
    return velocity.reshape(NTX, NTY, 2, CURVES, NODES)
```

```python
import math

import jax
import jax.numpy as jnp
import numpy as np
from jax import lax
from jax.experimental import pallas as pl
from jax.experimental.pallas import tpu as pltpu
from jax.sharding import PartitionSpec as P

NODES = 128
FINE = 512
PANEL = 16
REFINE = 4
CURVES = 8
PANELS = FINE // PANEL
WIDE = PANEL * REFINE
COLS = WIDE + PANEL
BLOCKS = FINE // 128


SOFT_SQ = 1e-08
HIGH = lax.Precision.HIGHEST
NT = (((1,), (1,)), ((), ()))


def extended_2(block, sides, width):
    for axis, dim in sides:
        count = lax.axis_size(axis)
        forward = [(i, i + 1) for i in range(count - 1)]
        forward.append((count - 1, 0))
        backward = [(target, source) for source, target in forward]
        low = lax.ppermute(
            lax.slice_in_dim(block, block.shape[dim] - width, None, axis=dim), axis, forward
        )
        high = lax.ppermute(lax.slice_in_dim(block, 0, width, axis=dim), axis, backward)
        block = jnp.concatenate([low, block, high], axis=dim)
    return block


def spectral_tables(coarse_count, fine_count):
    coarse_index = np.arange(coarse_count)[:, None, None]
    fine_index = np.arange(fine_count)[None, :, None]
    modes = np.arange(1, coarse_count // 2)[None, None, :]
    nyquist = coarse_count // 2
    offset = 2.0 * np.pi * (fine_index / fine_count - coarse_index / coarse_count)
    upsample_table = (
        1.0 + 2.0 * np.sum(np.cos(modes * offset), axis=-1) + np.cos(nyquist * offset[..., 0])
    ) / coarse_count
    derive_table = (
        -2.0 * np.sum(modes * np.sin(modes * offset), axis=-1)
        - nyquist * np.sin(nyquist * offset[..., 0])
    ) / coarse_count
    return (
        jnp.asarray(upsample_table, dtype=jnp.float32),
        jnp.asarray(derive_table, dtype=jnp.float32),
    )


def lagrange_weights(panel_nodes, refine_factor):
    weights_table = np.zeros((panel_nodes + 3, panel_nodes * refine_factor))
    for column in range(panel_nodes * refine_factor):
        fraction = column % refine_factor / refine_factor
        start_node = column // refine_factor
        weights_table[start_node, column] = -fraction * (fraction - 1.0) * (fraction - 2.0) / 6.0
        weights_table[start_node + 1, column] = (
            (fraction + 1.0) * (fraction - 1.0) * (fraction - 2.0) / 2.0
        )
        weights_table[start_node + 2, column] = (
            -(fraction + 1.0) * fraction * (fraction - 2.0) / 2.0
        )
        weights_table[start_node + 3, column] = (fraction + 1.0) * fraction * (fraction - 1.0) / 6.0
    return np.asarray(weights_table, dtype=np.float32)


def window_table():
    weights = lagrange_weights(PANEL, REFINE)
    table = np.zeros((4 * COLS, 128), dtype=np.float32)
    for comp in range(4):
        for node in range(PANEL + 3):
            table[comp * COLS : comp * COLS + WIDE, comp * 32 + node] = weights[node]
        for node in range(PANEL):
            table[comp * COLS + WIDE + node, comp * 32 + node + 1] = 1.0
    return jnp.asarray(table)


def inverse(value):
    guess = pl.reciprocal(value, approx=True)
    return guess * (2.0 - value * guess)


def upsample_all(ext_ref, up_ref, de_ref, fine_ref):
    rows = ext_ref.shape[0] * CURVES
    comps = [ext_ref[:, comp].reshape(rows, NODES) for comp in range(4)]
    up = up_ref[...]
    de = de_ref[...]
    speed = None
    for comp in range(2):
        fine_ref[comp] = jnp.dot(comps[comp], up, precision=HIGH, preferred_element_type=jnp.float32)
        tangent = jnp.dot(comps[comp], de, precision=HIGH, preferred_element_type=jnp.float32)
        speed = tangent * tangent if speed is None else speed + tangent * tangent
    speed = jnp.sqrt(speed) * (2.0 * math.pi / FINE)
    for comp in range(2, 4):
        fine_ref[comp] = speed * jnp.dot(
            comps[comp], up, precision=HIGH, preferred_element_type=jnp.float32
        )


def place_slot(slot, first, fine_ref, src_ref, win_ref):
    lane = lax.broadcasted_iota(jnp.int32, (CURVES, 128), 1)
    shifts = ((slot // 3 - 1).astype(jnp.float32), (slot % 3 - 1).astype(jnp.float32))
    parts = []
    for comp in range(4):
        value = fine_ref[comp, pl.ds(pl.multiple_of(slot * CURVES, CURVES), CURVES), :]
        if comp < 2:
            value = value + shifts[comp]
        parts.append([value[:, 128 * b : 128 * (b + 1)] for b in range(BLOCKS)])
    for comp in range(4):
        for b in range(BLOCKS):
            for c in range(CURVES):
                src_ref[first + c, comp * BLOCKS + b] = jnp.broadcast_to(
                    parts[comp][b][c : c + 1], (8, 128)
                )
    for n in range(PANELS):
        start = (n * PANEL - 1) % FINE
        b, offset = start // 128, start % 128
        row = None
        for comp in range(4):
            shift = (comp * 32 - offset) % 128
            piece = pltpu.roll(parts[comp][b], shift, 1) if shift else parts[comp][b]
            if offset + PANEL + 3 > 128:
                after = parts[comp][(b + 1) % BLOCKS]
                after = pltpu.roll(after, shift, 1) if shift else after
                piece = jnp.where(lane - comp * 32 < 128 - offset, piece, after)
            row = piece if row is None else jnp.where(lane < comp * 32, row, piece)
        win_ref[pl.ds(slot * CURVES * PANELS + n, CURVES, stride=PANELS), :] = row


def pair_terms(tx, ty, px, py, gx, gy):
    rx = tx - px
    ry = ty - py
    dist_sq = rx * rx + ry * ry + SOFT_SQ
    logs = jnp.log(dist_sq)
    proj = (rx * gx + ry * gy) * inverse(dist_sq)
    return proj * rx, proj * ry, logs * gx, logs * gy


GROUP = 4


def curve_velocity(pos_x, pos_y, live, src_ref, tgt_ref, acc_ref):
    tgt_ref[0] = jnp.broadcast_to(pos_x, (128, 128)).T
    tgt_ref[1] = jnp.broadcast_to(pos_y, (128, 128)).T

    @pl.loop(0, NODES // (8 * GROUP))
    def block(t):
        first = pl.multiple_of(t * 8 * GROUP, 8 * GROUP)
        txs = [tgt_ref[0, pl.ds(first + 8 * i, 8), :] for i in range(GROUP)]
        tys = [tgt_ref[1, pl.ds(first + 8 * i, 8), :] for i in range(GROUP)]

        def visit(k, accs):
            accs = list(accs)
            for b in range(BLOCKS):
                px, py, gx, gy = (src_ref[k, comp * BLOCKS + b] for comp in range(4))
                for i in range(GROUP):
                    terms = pair_terms(txs[i], tys[i], px, py, gx, gy)
                    for j in range(4):
                        accs[4 * i + j] = accs[4 * i + j] + terms[j]
            return tuple(accs)

        zero = jnp.zeros((8, 128), jnp.float32)
        accs = lax.fori_loop(0, live, visit, (zero,) * (4 * GROUP))
        for i in range(GROUP):
            for d in range(2):
                acc_ref[d, pl.ds(first + 8 * i, 8), :] = accs[4 * i + d] - 0.5 * accs[4 * i + 2 + d]

    return [jnp.sum(acc_ref[d].T, axis=0, keepdims=True) for d in range(2)]


def kernel(
    count_ref, panel_ref, ext_ref, goal_ref, up_ref, de_ref, mix_ref, out_ref,
    fine_ref, src_ref, win_ref, tgt_ref, acc_ref, near_ref,
):
    upsample_all(ext_ref, up_ref, de_ref, fine_ref)

    def place(slot, first):
        place_slot(slot, first, fine_ref, src_ref, win_ref)
        return first + count_ref[slot]

    live = lax.fori_loop(0, 9, place, 0)
    own = count_ref[4]
    out_ref[...] = jnp.zeros_like(out_ref)

    @pl.loop(0, own)
    def curve(c):
        vel = curve_velocity(
            ext_ref[4, 0, pl.ds(c, 1), :], ext_ref[4, 1, pl.ds(c, 1), :], live,
            src_ref, tgt_ref, acc_ref,
        )
        for d in range(2):
            out_ref[d, pl.ds(c, 1), :] = vel[d]

    near_count = count_ref[9]

    @pl.loop(0, (near_count + 127) // 128)
    def chunk(q):
        @pl.loop(0, 16)
        def fetch(h):
            for j in range(8):
                near_ref[pl.ds(h * 8 + j, 1), :] = win_ref[pl.ds(panel_ref[q * 128 + h * 8 + j], 1), :]

        mixed = lax.dot_general(
            mix_ref[...], near_ref[...], NT, precision=HIGH, preferred_element_type=jnp.float32
        )
        goal = goal_ref[pl.ds(q, 1), :]
        node = lax.broadcasted_iota(jnp.int32, (128, 128), 0)
        hot = (node == goal % NODES).astype(jnp.float32)
        curve_row = lax.broadcasted_iota(jnp.int32, (CURVES, 128), 0) == goal // NODES
        points = []
        for d in range(2):
            every = jnp.dot(ext_ref[4, d], hot, precision=HIGH, preferred_element_type=jnp.float32)
            points.append(jnp.sum(jnp.where(curve_row, every, 0.0), axis=0, keepdims=True))
        terms = pair_terms(
            points[0], points[1], *(mixed[comp * COLS : (comp + 1) * COLS] for comp in range(4))
        )
        entry = q * 128 + lax.broadcasted_iota(jnp.int32, (1, 128), 1)
        for d in range(2):
            both = terms[d] - 0.5 * terms[2 + d]
            corr = 0.25 * jnp.sum(both[:WIDE], axis=0, keepdims=True) - jnp.sum(
                both[WIDE:], axis=0, keepdims=True
            )
            corr = jnp.where(entry < near_count, corr, 0.0)
            spread = jnp.where(curve_row, corr, 0.0)
            out_ref[d] += lax.dot_general(
                spread, hot, NT, precision=HIGH, preferred_element_type=jnp.float32
            )

    alive = lax.broadcasted_iota(jnp.int32, (CURVES, NODES), 0) < own
    for d in range(2):
        out_ref[d] = jnp.where(alive, out_ref[d], 0.0)


def body(curves, curve_counts, near_counts, near_lists):
    upsample_table, derive_table = spectral_tables(NODES, FINE)
    curve_count = curve_counts[0, 0]
    living = jnp.arange(CURVES, dtype=jnp.int32) < curve_count
    masked = jnp.concatenate(
        [
            curves[:, :, 0:2],
            jnp.where(living[:, None], curves[:, :, 2:4], 0.0),
            jnp.broadcast_to(curve_counts[:, :, None, None, None].astype(jnp.float32), (1, 1, 1, CURVES, NODES)),
        ],
        axis=2,
    )
    extended = extended_2(masked, (("gx", 0), ("gy", 1)), 1).reshape(9, 5, CURVES, NODES)
    counts = jnp.concatenate([extended[:, 4, 0, 0].astype(jnp.int32), near_counts[0]])
    near = near_lists.shape[-1]
    smem = pl.BlockSpec(memory_space=pltpu.SMEM)
    vmem = pl.BlockSpec(memory_space=pltpu.VMEM)
    velocity = pl.pallas_call(
        kernel,
        name="near_field",
        out_shape=jax.ShapeDtypeStruct((2, CURVES, NODES), jnp.float32),
        in_specs=[smem, smem] + [vmem] * 5,
        out_specs=vmem,
        scratch_shapes=[
            pltpu.VMEM((4, 9 * CURVES, FINE), jnp.float32),
            pltpu.VMEM((10 * CURVES, 4 * BLOCKS, 8, 128), jnp.float32),
            pltpu.VMEM((9 * CURVES * PANELS, 128), jnp.float32),
            pltpu.VMEM((2, 128, 128), jnp.float32),
            pltpu.VMEM((2, 128, 128), jnp.float32),
            pltpu.VMEM((128, 128), jnp.float32),
        ],
        compiler_params=pltpu.CompilerParams(vmem_limit_bytes=32 * 1024 * 1024),
    )(
        counts,
        near_lists[0, 0, 1],
        extended,
        near_lists[0, 0, 0].reshape(near // 128, 128),
        upsample_table,
        derive_table,
        window_table(),
    )
    return velocity[None, None]


def solution(mesh):
    in_specs = (
        P("gx", "gy", None, None, None),
        P("gx", "gy"),
        P("gx", "gy"),
        P("gx", "gy", None, None),
    )
    out_specs = P("gx", "gy", None, None, None)
    return jax.shard_map(body, mesh=mesh, in_specs=in_specs, out_specs=out_specs, check_vma=False)
```

```python
import math

import jax
import jax.numpy as jnp
import numpy as np
from jax import lax
from jax.experimental import pallas as pl
from jax.experimental.pallas import tpu as pltpu
from jax.sharding import PartitionSpec as P

NODES = 128
FINE = 512
PANEL = 16
REFINE = 4
CURVES = 8
PANELS = FINE // PANEL
WIDE = PANEL * REFINE
COLS = WIDE + PANEL
BLOCKS = FINE // 128


SOFT_SQ = 1e-08
HIGH = lax.Precision.HIGHEST
NT = (((1,), (1,)), ((), ()))


def spectral_tables(coarse_count, fine_count):
    coarse_index = np.arange(coarse_count)[:, None, None]
    fine_index = np.arange(fine_count)[None, :, None]
    modes = np.arange(1, coarse_count // 2)[None, None, :]
    nyquist = coarse_count // 2
    offset = 2.0 * np.pi * (fine_index / fine_count - coarse_index / coarse_count)
    upsample_table = (
        1.0 + 2.0 * np.sum(np.cos(modes * offset), axis=-1) + np.cos(nyquist * offset[..., 0])
    ) / coarse_count
    derive_table = (
        -2.0 * np.sum(modes * np.sin(modes * offset), axis=-1)
        - nyquist * np.sin(nyquist * offset[..., 0])
    ) / coarse_count
    return (
        jnp.asarray(upsample_table, dtype=jnp.float32),
        jnp.asarray(derive_table, dtype=jnp.float32),
    )


def lagrange_weights(panel_nodes, refine_factor):
    weights_table = np.zeros((panel_nodes + 3, panel_nodes * refine_factor))
    for column in range(panel_nodes * refine_factor):
        fraction = column % refine_factor / refine_factor
        start_node = column // refine_factor
        weights_table[start_node, column] = -fraction * (fraction - 1.0) * (fraction - 2.0) / 6.0
        weights_table[start_node + 1, column] = (
            (fraction + 1.0) * (fraction - 1.0) * (fraction - 2.0) / 2.0
        )
        weights_table[start_node + 2, column] = (
            -(fraction + 1.0) * fraction * (fraction - 2.0) / 2.0
        )
        weights_table[start_node + 3, column] = (fraction + 1.0) * fraction * (fraction - 1.0) / 6.0
    return np.asarray(weights_table, dtype=np.float32)


def window_table():
    weights = lagrange_weights(PANEL, REFINE)
    table = np.zeros((4 * COLS, 128), dtype=np.float32)
    for comp in range(4):
        for node in range(PANEL + 3):
            table[comp * COLS : comp * COLS + WIDE, comp * 32 + node] = weights[node]
        for node in range(PANEL):
            table[comp * COLS + WIDE + node, comp * 32 + node + 1] = 1.0
    return jnp.asarray(table)


def inverse(value):
    guess = pl.reciprocal(value, approx=True)
    return guess * (2.0 - value * guess)


def upsample_all(halo_ref, up_ref, de_ref, fine_ref):
    rows = halo_ref.shape[0] * CURVES
    comps = [
        halo_ref[:, comp * CURVES : (comp + 1) * CURVES, :].reshape(rows, NODES)
        for comp in range(4)
    ]
    up = up_ref[...]
    de = de_ref[...]
    speed = None
    for comp in range(2):
        fine_ref[comp] = jnp.dot(comps[comp], up, precision=HIGH, preferred_element_type=jnp.float32)
        tangent = jnp.dot(comps[comp], de, precision=HIGH, preferred_element_type=jnp.float32)
        speed = tangent * tangent if speed is None else speed + tangent * tangent
    speed = jnp.sqrt(speed) * (2.0 * math.pi / FINE)
    for comp in range(2, 4):
        fine_ref[comp] = speed * jnp.dot(
            comps[comp], up, precision=HIGH, preferred_element_type=jnp.float32
        )


def fine_blocks(fine_ref, tile):
    parts = []
    for comp in range(4):
        value = fine_ref[comp, pl.ds(pl.multiple_of(tile * CURVES, CURVES), CURVES), :]
        parts.append([value[:, 128 * b : 128 * (b + 1)] for b in range(BLOCKS)])
    return parts


def place_sources(tile, fine_ref, src_ref):
    parts = fine_blocks(fine_ref, tile)
    for comp in range(4):
        for b in range(BLOCKS):
            for c in range(CURVES):
                src_ref[tile * CURVES + c, comp * BLOCKS + b] = jnp.broadcast_to(
                    parts[comp][b][c : c + 1], (8, 128)
                )


def place_windows(slot, tile, fine_ref, win_ref):
    lane = lax.broadcasted_iota(jnp.int32, (CURVES, 128), 1)
    shifts = ((slot // 3 - 1).astype(jnp.float32), (slot % 3 - 1).astype(jnp.float32))
    parts = fine_blocks(fine_ref, tile)
    for comp in range(2):
        parts[comp] = [value + shifts[comp] for value in parts[comp]]
    for n in range(PANELS):
        start = (n * PANEL - 1) % FINE
        b, offset = start // 128, start % 128
        row = None
        for comp in range(4):
            shift = (comp * 32 - offset) % 128
            piece = pltpu.roll(parts[comp][b], shift, 1) if shift else parts[comp][b]
            if offset + PANEL + 3 > 128:
                after = parts[comp][(b + 1) % BLOCKS]
                after = pltpu.roll(after, shift, 1) if shift else after
                piece = jnp.where(lane - comp * 32 < 128 - offset, piece, after)
            row = piece if row is None else jnp.where(lane < comp * 32, row, piece)
        win_ref[pl.ds(slot * CURVES * PANELS + n, CURVES, stride=PANELS), :] = row


def pair_terms(tx, ty, px, py, gx, gy):
    rx = tx - px
    ry = ty - py
    dist_sq = rx * rx + ry * ry + SOFT_SQ
    logs = jnp.log(dist_sq)
    proj = (rx * gx + ry * gy) * inverse(dist_sq)
    return proj * rx, proj * ry, logs * gx, logs * gy


GROUP = 4


def curve_velocity(pos_x, pos_y, first, last, src_ref, row_ref, move_ref, tgt_ref, acc_ref):
    tgt_ref[0] = jnp.broadcast_to(pos_x, (128, 128)).T
    tgt_ref[1] = jnp.broadcast_to(pos_y, (128, 128)).T

    @pl.loop(0, NODES // (8 * GROUP))
    def block(t):
        base = pl.multiple_of(t * 8 * GROUP, 8 * GROUP)
        txs = [tgt_ref[0, pl.ds(base + 8 * i, 8), :] for i in range(GROUP)]
        tys = [tgt_ref[1, pl.ds(base + 8 * i, 8), :] for i in range(GROUP)]

        def visit(k, accs):
            accs = list(accs)
            row = row_ref[k]
            for b in range(BLOCKS):
                px, py, gx, gy = (src_ref[row, comp * BLOCKS + b] for comp in range(4))
                px = px + move_ref[0, k]
                py = py + move_ref[1, k]
                for i in range(GROUP):
                    terms = pair_terms(txs[i], tys[i], px, py, gx, gy)
                    for j in range(4):
                        accs[4 * i + j] = accs[4 * i + j] + terms[j]
            return tuple(accs)

        zero = jnp.zeros((8, 128), jnp.float32)
        accs = lax.fori_loop(first, last, visit, (zero,) * (4 * GROUP))
        for i in range(GROUP):
            for d in range(2):
                acc_ref[d, pl.ds(base + 8 * i, 8), :] = accs[4 * i + d] - 0.5 * accs[4 * i + 2 + d]

    return [jnp.sum(acc_ref[d].T, axis=0, keepdims=True) for d in range(2)]


BX = 4
BY = 2
MEMBERS = BX * BY
NEAR_COST = 4
PACK = 5 * CURVES
MESH = pl.DeviceIdType.MESH


def halo_cols(size):
    return BY if size == BY else BY + 2


def halo_col(local, cols):
    return local % BY if cols == BY else local + 1


def tile_at(ti, tj, slot, cols):
    return (ti + slot // 3) * cols + halo_col(tj + slot % 3 - 1 + (BY if cols == BY else 0), cols)


def gather_kernel(nx, ny, curves_ref, alive_ref, near_ref, halo_ref, send_sem, recv_sem):
    cols = halo_cols(ny)
    wide = cols > BY
    i, j = lax.axis_index("gx"), lax.axis_index("gy")
    gi, li, gj, lj = i // BX, i % BX, j // BY, j % BY
    own_row, own_col = li + 1, halo_col(lj, cols)
    me = li * BY + lj
    edge = jnp.where((li == 0) | (li == BX - 1), 1, 0)
    to_gi = gi + jnp.where(li == 0, -1, 1)
    to_row = jnp.where(li == 0, BX + 1, 0)
    to_gj = gj + jnp.where(lj == 0, -1, 1)
    to_col = jnp.where(lj == 0, BY + 1, 0)

    def device(x, y):
        return ((x + nx) % nx, (y + ny) % ny)

    def member(bx, by, t):
        return device(bx * BX + t // BY, by * BY + t % BY)

    outer = [(r, c) for r in (0, BX + 1) for c in range(cols)]
    if wide:
        outer += [(r, c) for r in range(1, BX + 1) for c in (0, BY + 1)]

    barrier = pltpu.get_barrier_semaphore()
    for t in range(1, MEMBERS):
        pl.semaphore_signal(
            barrier, inc=1, device_id=member(gi, gj, (me + t) % MEMBERS), device_id_type=MESH
        )
    for r, c in outer:
        pl.semaphore_signal(
            barrier,
            inc=1,
            device_id=device(gi * BX + r - 1, gj * BY + c - (1 if wide else 0)),
            device_id_type=MESH,
        )

    living = lax.broadcasted_iota(jnp.int32, (CURVES, NODES), 0) < alive_ref[...]
    for comp in range(4):
        value = curves_ref[comp]
        halo_ref[own_row, own_col, comp * CURVES : (comp + 1) * CURVES, :] = (
            value if comp < 2 else jnp.where(living, value, 0.0)
        )
    numbers = jnp.where(
        lax.broadcasted_iota(jnp.int32, (CURVES, NODES), 0) == 0, alive_ref[...], near_ref[...]
    )
    halo_ref[own_row, own_col, 4 * CURVES :, :] = numbers.astype(jnp.float32)

    scale = 2 if wide else 1
    pl.semaphore_wait(barrier, MEMBERS * scale - 1 + edge * (MEMBERS * scale))

    def copy(kind, t, row, col, target):
        return pltpu.make_async_remote_copy(
            src_ref=halo_ref.at[own_row, own_col],
            dst_ref=halo_ref.at[row, col],
            send_sem=send_sem.at[kind, t],
            recv_sem=recv_sem.at[row, col],
            device_id=target,
            device_id_type=MESH,
        )

    always = [
        copy(0, t, own_row, own_col, member(gi, gj, (me + t) % MEMBERS))
        for t in range(1, MEMBERS)
    ]
    edges = [copy(1, t, to_row, own_col, member(to_gi, gj, t)) for t in range(MEMBERS)]
    if wide:
        always += [copy(2, t, own_row, to_col, member(gi, to_gj, t)) for t in range(MEMBERS)]
        edges += [copy(3, t, to_row, to_col, member(to_gi, to_gj, t)) for t in range(MEMBERS)]

    @pl.when(edge == 1)
    def _():
        for item in edges:
            item.start()

    for item in always:
        item.start()

    other = member(gi, gj, (me + 1) % MEMBERS)
    for t in range(1, MEMBERS):
        source = (me + t) % MEMBERS
        copy(0, t, source // BY + 1, halo_col(source % BY, cols), other).wait_recv()
    for r, c in outer:
        copy(0, 1, r, c, other).wait_recv()
    for item in always:
        item.wait_send()

    @pl.when(edge == 1)
    def _():
        for item in edges:
            item.wait_send()


def return_kernel(nx, ny, part_ref, alive_ref, out_ref, got_ref, send_sem, recv_sem):
    i, j = lax.axis_index("gx"), lax.axis_index("gy")
    gi, gj = i // BX, j // BY
    me = i % BX * BY + j % BY

    def member(t):
        return (gi * BX + t // BY, gj * BY + t % BY)

    barrier = pltpu.get_barrier_semaphore()
    for t in range(1, MEMBERS):
        pl.semaphore_signal(
            barrier, inc=1, device_id=member((me + t) % MEMBERS), device_id_type=MESH
        )
    pl.semaphore_wait(barrier, MEMBERS - 1)
    copies = []
    for t in range(1, MEMBERS):
        target = (me + t) % MEMBERS
        copies.append(
            pltpu.make_async_remote_copy(
                src_ref=part_ref.at[target],
                dst_ref=got_ref.at[t],
                send_sem=send_sem.at[t],
                recv_sem=recv_sem.at[t],
                device_id=member(target),
                device_id_type=MESH,
            )
        )
        copies[-1].start()
    total = part_ref[me]
    for t in range(1, MEMBERS):
        copies[t - 1].wait_recv()
        total = total + got_ref[t]
    alive = lax.broadcasted_iota(jnp.int32, (CURVES, NODES), 0) < alive_ref[...]
    for d in range(2):
        out_ref[d] = jnp.where(alive, total[d], 0.0)
    for item in copies:
        item.wait_send()


def field_kernel(
    cols, count_ref, panel_ref, halo_ref, goal_ref, up_ref, de_ref, mix_ref, out_ref,
    fine_ref, src_ref, win_ref, tgt_ref, acc_ref, near_ref, work_ref, row_ref, move_ref,
):
    li, lj = lax.axis_index("gx") % BX, lax.axis_index("gy") % BY
    me = li * BY + lj
    upsample_all(halo_ref, up_ref, de_ref, fine_ref)
    out_ref[...] = jnp.zeros_like(out_ref)

    @pl.loop(0, (BX + 2) * cols)
    def place(tile):
        place_sources(tile, fine_ref, src_ref)

    @pl.loop(0, 9)
    def windows(slot):
        place_windows(slot, tile_at(li, lj, slot, cols), fine_ref, win_ref)

    def survey(t, carry):
        pairs, near = carry
        own = tile_at(t // BY, t % BY, 4, cols)
        sources = 0
        for slot in range(9):
            sources = sources + count_ref[2 * tile_at(t // BY, t % BY, slot, cols)]
        cost = (count_ref[2 * own + 1] + 127) // 128 * NEAR_COST
        work_ref[0, t] = sources
        work_ref[1, t] = pairs
        work_ref[2, t] = cost
        return pairs + sources * count_ref[2 * own], near + cost

    pairs, near = lax.fori_loop(0, MEMBERS, survey, (0, 0))
    quota = (pairs + near + MEMBERS - 1) // MEMBERS
    low = lax.fori_loop(
        0, me, lambda t, total: total + jnp.maximum(quota - work_ref[2, t], 0), 0
    )
    high = jnp.minimum(low + jnp.maximum(quota - work_ref[2, me], 0), pairs)
    low = jnp.minimum(low, pairs)

    @pl.loop(0, MEMBERS)
    def member(t):
        ti, tj = t // BY, t % BY
        own = tile_at(ti, tj, 4, cols)
        sources, base, curves = work_ref[0, t], work_ref[1, t], count_ref[2 * own]

        @pl.when((low < base + sources * curves) & (high > base))
        def _():
            def enlist(slot, first):
                tile = tile_at(ti, tj, slot, cols)
                for c in range(CURVES):
                    row_ref[first + c] = tile * CURVES + c
                    move_ref[0, first + c] = (slot // 3 - 1).astype(jnp.float32)
                    move_ref[1, first + c] = (slot % 3 - 1).astype(jnp.float32)
                return first + count_ref[2 * tile]

            lax.fori_loop(0, 9, enlist, 0)

            @pl.loop(0, curves)
            def curve(c):
                first = jnp.clip(low - base - c * sources, 0, sources)
                last = jnp.clip(high - base - c * sources, 0, sources)

                @pl.when(first < last)
                def _():
                    vel = curve_velocity(
                        halo_ref[own, pl.ds(c, 1), :], halo_ref[own, pl.ds(CURVES + c, 1), :],
                        first, last, src_ref, row_ref, move_ref, tgt_ref, acc_ref,
                    )
                    for d in range(2):
                        out_ref[t, d, pl.ds(c, 1), :] = vel[d]

    own = tile_at(li, lj, 4, cols)
    near_count = count_ref[2 * own + 1]

    @pl.loop(0, (near_count + 127) // 128)
    def chunk(q):
        @pl.loop(0, 16)
        def fetch(h):
            for j in range(8):
                near_ref[pl.ds(h * 8 + j, 1), :] = win_ref[pl.ds(panel_ref[q * 128 + h * 8 + j], 1), :]

        mixed = lax.dot_general(
            mix_ref[...], near_ref[...], NT, precision=HIGH, preferred_element_type=jnp.float32
        )
        goal = goal_ref[pl.ds(q, 1), :]
        node = lax.broadcasted_iota(jnp.int32, (128, 128), 0)
        hot = (node == goal % NODES).astype(jnp.float32)
        curve_row = lax.broadcasted_iota(jnp.int32, (CURVES, 128), 0) == goal // NODES
        points = []
        for d in range(2):
            every = jnp.dot(
                halo_ref[own, d * CURVES : (d + 1) * CURVES, :], hot,
                precision=HIGH, preferred_element_type=jnp.float32,
            )
            points.append(jnp.sum(jnp.where(curve_row, every, 0.0), axis=0, keepdims=True))
        terms = pair_terms(
            points[0], points[1], *(mixed[comp * COLS : (comp + 1) * COLS] for comp in range(4))
        )
        entry = q * 128 + lax.broadcasted_iota(jnp.int32, (1, 128), 1)
        for d in range(2):
            both = terms[d] - 0.5 * terms[2 + d]
            corr = 0.25 * jnp.sum(both[:WIDE], axis=0, keepdims=True) - jnp.sum(
                both[WIDE:], axis=0, keepdims=True
            )
            corr = jnp.where(entry < near_count, corr, 0.0)
            spread = jnp.where(curve_row, corr, 0.0)
            out_ref[me, d] += lax.dot_general(
                spread, hot, NT, precision=HIGH, preferred_element_type=jnp.float32
            )


def make_body(nx, ny):
    cols = halo_cols(ny)
    tiles = (BX + 2) * cols
    smem = pl.BlockSpec(memory_space=pltpu.SMEM)
    vmem = pl.BlockSpec(memory_space=pltpu.VMEM)

    def body(curves, curve_counts, near_counts, near_lists):
        upsample_table, derive_table = spectral_tables(NODES, FINE)
        near = near_lists.shape[-1]
        halo = pl.pallas_call(
            lambda *refs: gather_kernel(nx, ny, *refs),
            name="gather",
            out_shape=jax.ShapeDtypeStruct((BX + 2, cols, PACK, NODES), jnp.float32),
            in_specs=[vmem] * 3,
            out_specs=vmem,
            scratch_shapes=[
                pltpu.SemaphoreType.DMA((4, MEMBERS)),
                pltpu.SemaphoreType.DMA((BX + 2, cols)),
            ],
            compiler_params=pltpu.CompilerParams(collective_id=0, has_side_effects=True),
        )(curves[0, 0], curve_counts, near_counts)
        halo = halo.reshape(tiles, PACK, NODES)
        counts = halo[:, 4 * CURVES : 4 * CURVES + 2, 0].astype(jnp.int32).reshape(-1)
        part = pl.pallas_call(
            lambda *refs: field_kernel(cols, *refs),
            name="near_field",
            out_shape=jax.ShapeDtypeStruct((MEMBERS, 2, CURVES, NODES), jnp.float32),
            in_specs=[smem, smem] + [vmem] * 5,
            out_specs=vmem,
            scratch_shapes=[
                pltpu.VMEM((4, tiles * CURVES, FINE), jnp.float32),
                pltpu.VMEM((tiles * CURVES, 4 * BLOCKS, 8, 128), jnp.float32),
                pltpu.VMEM((9 * CURVES * PANELS, 128), jnp.float32),
                pltpu.VMEM((2, 128, 128), jnp.float32),
                pltpu.VMEM((2, 128, 128), jnp.float32),
                pltpu.VMEM((128, 128), jnp.float32),
                pltpu.SMEM((3, MEMBERS), jnp.int32),
                pltpu.SMEM((10 * CURVES,), jnp.int32),
                pltpu.SMEM((2, 10 * CURVES), jnp.float32),
            ],
            compiler_params=pltpu.CompilerParams(vmem_limit_bytes=40 * 1024 * 1024),
        )(
            counts,
            near_lists[0, 0, 1],
            halo,
            near_lists[0, 0, 0].reshape(near // 128, 128),
            upsample_table,
            derive_table,
            window_table(),
        )
        velocity = pl.pallas_call(
            lambda *refs: return_kernel(nx, ny, *refs),
            name="give_back",
            out_shape=jax.ShapeDtypeStruct((2, CURVES, NODES), jnp.float32),
            in_specs=[vmem] * 2,
            out_specs=vmem,
            scratch_shapes=[
                pltpu.VMEM((MEMBERS, 2, CURVES, NODES), jnp.float32),
                pltpu.SemaphoreType.DMA((MEMBERS,)),
                pltpu.SemaphoreType.DMA((MEMBERS,)),
            ],
            compiler_params=pltpu.CompilerParams(collective_id=1, has_side_effects=True),
        )(part, curve_counts)
        return velocity[None, None]

    return body


def solution(mesh):
    in_specs = (
        P("gx", "gy", None, None, None),
        P("gx", "gy"),
        P("gx", "gy"),
        P("gx", "gy", None, None),
    )
    out_specs = P("gx", "gy", None, None, None)
    body = make_body(mesh.shape["gx"], mesh.shape["gy"])
    return jax.shard_map(body, mesh=mesh, in_specs=in_specs, out_specs=out_specs, check_vma=False)
```

```python
import math

import jax
import jax.numpy as jnp
import numpy as np
from jax import lax
from jax.experimental import pallas as pl
from jax.experimental.pallas import tpu as pltpu
from jax.sharding import PartitionSpec as P

NODES = 128
FINE = 512
PANEL = 16
REFINE = 4
CURVES = 8
PANELS = FINE // PANEL
WIDE = PANEL * REFINE
COLS = WIDE + PANEL
BLOCKS = FINE // 128


SOFT_SQ = 1e-08
HIGH = lax.Precision.HIGHEST
NT = (((1,), (1,)), ((), ()))


def spectral_tables(coarse_count, fine_count):
    coarse_index = np.arange(coarse_count)[:, None, None]
    fine_index = np.arange(fine_count)[None, :, None]
    modes = np.arange(1, coarse_count // 2)[None, None, :]
    nyquist = coarse_count // 2
    offset = 2.0 * np.pi * (fine_index / fine_count - coarse_index / coarse_count)
    upsample_table = (
        1.0 + 2.0 * np.sum(np.cos(modes * offset), axis=-1) + np.cos(nyquist * offset[..., 0])
    ) / coarse_count
    derive_table = (
        -2.0 * np.sum(modes * np.sin(modes * offset), axis=-1)
        - nyquist * np.sin(nyquist * offset[..., 0])
    ) / coarse_count
    return (
        jnp.asarray(upsample_table, dtype=jnp.float32),
        jnp.asarray(derive_table, dtype=jnp.float32),
    )


def lagrange_weights(panel_nodes, refine_factor):
    weights_table = np.zeros((panel_nodes + 3, panel_nodes * refine_factor))
    for column in range(panel_nodes * refine_factor):
        fraction = column % refine_factor / refine_factor
        start_node = column // refine_factor
        weights_table[start_node, column] = -fraction * (fraction - 1.0) * (fraction - 2.0) / 6.0
        weights_table[start_node + 1, column] = (
            (fraction + 1.0) * (fraction - 1.0) * (fraction - 2.0) / 2.0
        )
        weights_table[start_node + 2, column] = (
            -(fraction + 1.0) * fraction * (fraction - 2.0) / 2.0
        )
        weights_table[start_node + 3, column] = (fraction + 1.0) * fraction * (fraction - 1.0) / 6.0
    return np.asarray(weights_table, dtype=np.float32)


def window_table():
    weights = lagrange_weights(PANEL, REFINE)
    table = np.zeros((4 * COLS, 128), dtype=np.float32)
    for comp in range(4):
        for node in range(PANEL + 3):
            table[comp * COLS : comp * COLS + WIDE, comp * 32 + node] = weights[node]
        for node in range(PANEL):
            table[comp * COLS + WIDE + node, comp * 32 + node + 1] = 1.0
    return jnp.asarray(table)


def upsample_all(halo_ref, up_ref, de_ref, fine_ref):
    rows = halo_ref.shape[0] * CURVES
    comps = [
        halo_ref[:, comp * CURVES : (comp + 1) * CURVES, :].reshape(rows, NODES)
        for comp in range(4)
    ]
    up = up_ref[...]
    de = de_ref[...]
    speed = None
    for comp in range(2):
        fine_ref[comp] = jnp.dot(comps[comp], up, precision=HIGH, preferred_element_type=jnp.float32)
        tangent = jnp.dot(comps[comp], de, precision=HIGH, preferred_element_type=jnp.float32)
        speed = tangent * tangent if speed is None else speed + tangent * tangent
    speed = jnp.sqrt(speed) * (2.0 * math.pi / FINE)
    for comp in range(2, 4):
        fine_ref[comp] = speed * jnp.dot(
            comps[comp], up, precision=HIGH, preferred_element_type=jnp.float32
        )


def fine_blocks(fine_ref, tile):
    parts = []
    for comp in range(4):
        value = fine_ref[comp, pl.ds(pl.multiple_of(tile * CURVES, CURVES), CURVES), :]
        parts.append([value[:, 128 * b : 128 * (b + 1)] for b in range(BLOCKS)])
    return parts


def place_sources(tile, fine_ref, src_ref):
    parts = fine_blocks(fine_ref, tile)
    for comp in range(4):
        for b in range(BLOCKS):
            for c in range(CURVES):
                src_ref[tile * CURVES + c, comp * BLOCKS + b] = jnp.broadcast_to(
                    parts[comp][b][c : c + 1], (8, 128)
                )


def place_windows(slot, tile, fine_ref, win_ref):
    lane = lax.broadcasted_iota(jnp.int32, (CURVES, 128), 1)
    shifts = ((slot // 3 - 1).astype(jnp.float32), (slot % 3 - 1).astype(jnp.float32))
    parts = fine_blocks(fine_ref, tile)
    for comp in range(2):
        parts[comp] = [value + shifts[comp] for value in parts[comp]]
    for n in range(PANELS):
        start = (n * PANEL - 1) % FINE
        b, offset = start // 128, start % 128
        row = None
        for comp in range(4):
            shift = (comp * 32 - offset) % 128
            piece = pltpu.roll(parts[comp][b], shift, 1) if shift else parts[comp][b]
            if offset + PANEL + 3 > 128:
                after = parts[comp][(b + 1) % BLOCKS]
                after = pltpu.roll(after, shift, 1) if shift else after
                piece = jnp.where(lane - comp * 32 < 128 - offset, piece, after)
            row = piece if row is None else jnp.where(lane < comp * 32, row, piece)
        win_ref[pl.ds(slot * CURVES * PANELS + n, CURVES, stride=PANELS), :] = row


def pair_terms(tx, ty, px, py, gx, gy):
    rx = tx - px
    ry = ty - py
    dist_sq = rx * rx + ry * ry + SOFT_SQ
    logs = jnp.log(dist_sq)
    proj = (rx * gx + ry * gy) * (1.0 / dist_sq)
    return proj * rx, proj * ry, logs * gx, logs * gy


GROUP = 8


def curve_velocity(pos_x, pos_y, first, last, src_ref, row_ref, move_ref, tgt_ref, acc_ref):
    tgt_ref[0] = jnp.broadcast_to(pos_x, (128, 128)).T
    tgt_ref[1] = jnp.broadcast_to(pos_y, (128, 128)).T

    @pl.loop(0, NODES // (8 * GROUP))
    def block(t):
        base = pl.multiple_of(t * 8 * GROUP, 8 * GROUP)
        txs = [tgt_ref[0, pl.ds(base + 8 * i, 8), :] for i in range(GROUP)]
        tys = [tgt_ref[1, pl.ds(base + 8 * i, 8), :] for i in range(GROUP)]

        def visit(k, accs):
            accs = list(accs)
            row = row_ref[k]
            for b in range(BLOCKS):
                px, py, gx, gy = (src_ref[row, comp * BLOCKS + b] for comp in range(4))
                px = px + move_ref[0, k]
                py = py + move_ref[1, k]
                for i in range(GROUP):
                    terms = pair_terms(txs[i], tys[i], px, py, gx, gy)
                    for j in range(4):
                        accs[4 * i + j] = accs[4 * i + j] + terms[j]
            return tuple(accs)

        zero = jnp.zeros((8, 128), jnp.float32)
        accs = lax.fori_loop(first, last, visit, (zero,) * (4 * GROUP))
        for i in range(GROUP):
            for d in range(2):
                acc_ref[d, pl.ds(base + 8 * i, 8), :] = accs[4 * i + d] - 0.5 * accs[4 * i + 2 + d]

    return [jnp.sum(acc_ref[d].T, axis=0, keepdims=True) for d in range(2)]


BX = 4
BY = 2
MEMBERS = BX * BY
NEAR_COST = 4
PACK = 5 * CURVES
MESH = pl.DeviceIdType.MESH


def halo_cols(size):
    return BY if size == BY else BY + 2


def halo_col(local, cols):
    return local % BY if cols == BY else local + 1


def tile_at(ti, tj, slot, cols):
    return (ti + slot // 3) * cols + halo_col(tj + slot % 3 - 1 + (BY if cols == BY else 0), cols)


def gather_kernel(nx, ny, curves_ref, alive_ref, near_ref, halo_ref, send_sem, recv_sem):
    cols = halo_cols(ny)
    wide = cols > BY
    i, j = lax.axis_index("gx"), lax.axis_index("gy")
    gi, li, gj, lj = i // BX, i % BX, j // BY, j % BY
    own_row, own_col = li + 1, halo_col(lj, cols)
    me = li * BY + lj
    edge = jnp.where((li == 0) | (li == BX - 1), 1, 0)
    to_gi = gi + jnp.where(li == 0, -1, 1)
    to_row = jnp.where(li == 0, BX + 1, 0)
    to_gj = gj + jnp.where(lj == 0, -1, 1)
    to_col = jnp.where(lj == 0, BY + 1, 0)

    def device(x, y):
        return ((x + nx) % nx, (y + ny) % ny)

    def member(bx, by, t):
        return device(bx * BX + t // BY, by * BY + t % BY)

    outer = [(r, c) for r in (0, BX + 1) for c in range(cols)]
    if wide:
        outer += [(r, c) for r in range(1, BX + 1) for c in (0, BY + 1)]

    barrier = pltpu.get_barrier_semaphore()
    for t in range(1, MEMBERS):
        pl.semaphore_signal(
            barrier, inc=1, device_id=member(gi, gj, (me + t) % MEMBERS), device_id_type=MESH
        )
    for r, c in outer:
        pl.semaphore_signal(
            barrier,
            inc=1,
            device_id=device(gi * BX + r - 1, gj * BY + c - (1 if wide else 0)),
            device_id_type=MESH,
        )

    living = lax.broadcasted_iota(jnp.int32, (CURVES, NODES), 0) < alive_ref[...]
    for comp in range(4):
        value = curves_ref[comp]
        halo_ref[own_row, own_col, comp * CURVES : (comp + 1) * CURVES, :] = (
            value if comp < 2 else jnp.where(living, value, 0.0)
        )
    numbers = jnp.where(
        lax.broadcasted_iota(jnp.int32, (CURVES, NODES), 0) == 0, alive_ref[...], near_ref[...]
    )
    halo_ref[own_row, own_col, 4 * CURVES :, :] = numbers.astype(jnp.float32)

    scale = 2 if wide else 1
    pl.semaphore_wait(barrier, MEMBERS * scale - 1 + edge * (MEMBERS * scale))

    def copy(kind, t, row, col, target):
        return pltpu.make_async_remote_copy(
            src_ref=halo_ref.at[own_row, own_col],
            dst_ref=halo_ref.at[row, col],
            send_sem=send_sem.at[kind, t],
            recv_sem=recv_sem.at[row, col],
            device_id=target,
            device_id_type=MESH,
        )

    always = [
        copy(0, t, own_row, own_col, member(gi, gj, (me + t) % MEMBERS))
        for t in range(1, MEMBERS)
    ]
    edges = [copy(1, t, to_row, own_col, member(to_gi, gj, t)) for t in range(MEMBERS)]
    if wide:
        always += [copy(2, t, own_row, to_col, member(gi, to_gj, t)) for t in range(MEMBERS)]
        edges += [copy(3, t, to_row, to_col, member(to_gi, to_gj, t)) for t in range(MEMBERS)]

    @pl.when(edge == 1)
    def _():
        for item in edges:
            item.start()

    for item in always:
        item.start()

    other = member(gi, gj, (me + 1) % MEMBERS)
    for t in range(1, MEMBERS):
        source = (me + t) % MEMBERS
        copy(0, t, source // BY + 1, halo_col(source % BY, cols), other).wait_recv()
    for r, c in outer:
        copy(0, 1, r, c, other).wait_recv()
    for item in always:
        item.wait_send()

    @pl.when(edge == 1)
    def _():
        for item in edges:
            item.wait_send()


def return_kernel(nx, ny, part_ref, alive_ref, out_ref, got_ref, send_sem, recv_sem):
    i, j = lax.axis_index("gx"), lax.axis_index("gy")
    gi, gj = i // BX, j // BY
    me = i % BX * BY + j % BY

    def member(t):
        return (gi * BX + t // BY, gj * BY + t % BY)

    barrier = pltpu.get_barrier_semaphore()
    for t in range(1, MEMBERS):
        pl.semaphore_signal(
            barrier, inc=1, device_id=member((me + t) % MEMBERS), device_id_type=MESH
        )
    pl.semaphore_wait(barrier, MEMBERS - 1)
    copies = []
    for t in range(1, MEMBERS):
        target = (me + t) % MEMBERS
        copies.append(
            pltpu.make_async_remote_copy(
                src_ref=part_ref.at[target],
                dst_ref=got_ref.at[t],
                send_sem=send_sem.at[t],
                recv_sem=recv_sem.at[t],
                device_id=member(target),
                device_id_type=MESH,
            )
        )
        copies[-1].start()
    total = part_ref[me]
    for t in range(1, MEMBERS):
        copies[t - 1].wait_recv()
        total = total + got_ref[t]
    alive = lax.broadcasted_iota(jnp.int32, (CURVES, NODES), 0) < alive_ref[...]
    for d in range(2):
        out_ref[d] = jnp.where(alive, total[d], 0.0)
    for item in copies:
        item.wait_send()


def field_kernel(
    cols, panel_ref, goal_ref, halo_hbm, up_hbm, de_hbm, mix_hbm, out_ref,
    halo_ref, up_ref, de_ref, mix_ref, number_ref,
    fine_ref, src_ref, win_ref, tgt_ref, acc_ref, near_ref, work_ref, row_ref, move_ref, count_ref, sem,
):
    tiles = (BX + 2) * cols
    loads = [
        pltpu.make_async_copy(source, target, sem.at[n])
        for n, (source, target) in enumerate(
            (
                (halo_hbm, halo_ref),
                (up_hbm, up_ref),
                (de_hbm, de_ref),
                (mix_hbm, mix_ref),
                (halo_hbm.at[:, pl.ds(4 * CURVES, CURVES), :], number_ref),
            )
        )
    ]
    for item in loads:
        item.start()
    for item in loads:
        item.wait()

    @pl.loop(0, tiles)
    def numbers(tile):
        for n in range(2):
            count_ref[2 * tile + n] = number_ref[tile, n, 0].astype(jnp.int32)

    li, lj = lax.axis_index("gx") % BX, lax.axis_index("gy") % BY
    me = li * BY + lj
    upsample_all(halo_ref, up_ref, de_ref, fine_ref)
    out_ref[...] = jnp.zeros_like(out_ref)

    @pl.loop(0, (BX + 2) * cols)
    def place(tile):
        place_sources(tile, fine_ref, src_ref)

    @pl.loop(0, 9)
    def windows(slot):
        place_windows(slot, tile_at(li, lj, slot, cols), fine_ref, win_ref)

    def survey(t, carry):
        pairs, near = carry
        own = tile_at(t // BY, t % BY, 4, cols)
        sources = 0
        for slot in range(9):
            sources = sources + count_ref[2 * tile_at(t // BY, t % BY, slot, cols)]
        cost = (count_ref[2 * own + 1] + 127) // 128 * NEAR_COST
        work_ref[0, t] = sources
        work_ref[1, t] = pairs
        work_ref[2, t] = cost
        return pairs + sources * count_ref[2 * own], near + cost

    pairs, near = lax.fori_loop(0, MEMBERS, survey, (0, 0))
    quota = (pairs + near + MEMBERS - 1) // MEMBERS
    low = lax.fori_loop(
        0, me, lambda t, total: total + jnp.maximum(quota - work_ref[2, t], 0), 0
    )
    high = jnp.minimum(low + jnp.maximum(quota - work_ref[2, me], 0), pairs)
    low = jnp.minimum(low, pairs)

    @pl.loop(0, MEMBERS)
    def member(t):
        ti, tj = t // BY, t % BY
        own = tile_at(ti, tj, 4, cols)
        sources, base, curves = work_ref[0, t], work_ref[1, t], count_ref[2 * own]

        @pl.when((low < base + sources * curves) & (high > base))
        def _():
            def enlist(slot, first):
                tile = tile_at(ti, tj, slot, cols)
                for c in range(CURVES):
                    row_ref[first + c] = tile * CURVES + c
                    move_ref[0, first + c] = (slot // 3 - 1).astype(jnp.float32)
                    move_ref[1, first + c] = (slot % 3 - 1).astype(jnp.float32)
                return first + count_ref[2 * tile]

            lax.fori_loop(0, 9, enlist, 0)

            @pl.loop(0, curves)
            def curve(c):
                first = jnp.clip(low - base - c * sources, 0, sources)
                last = jnp.clip(high - base - c * sources, 0, sources)

                @pl.when(first < last)
                def _():
                    vel = curve_velocity(
                        halo_ref[own, pl.ds(c, 1), :], halo_ref[own, pl.ds(CURVES + c, 1), :],
                        first, last, src_ref, row_ref, move_ref, tgt_ref, acc_ref,
                    )
                    for d in range(2):
                        out_ref[t, d, pl.ds(c, 1), :] = vel[d]

    own = tile_at(li, lj, 4, cols)
    near_count = count_ref[2 * own + 1]

    @pl.loop(0, (near_count + 127) // 128)
    def chunk(q):
        @pl.loop(0, 16)
        def fetch(h):
            for j in range(8):
                near_ref[pl.ds(h * 8 + j, 1), :] = win_ref[pl.ds(panel_ref[q * 128 + h * 8 + j], 1), :]

        mixed = lax.dot_general(
            mix_ref[...], near_ref[...], NT, precision=HIGH, preferred_element_type=jnp.float32
        )
        goal = goal_ref[pl.ds(q, 1), :]
        node = lax.broadcasted_iota(jnp.int32, (128, 128), 0)
        hot = (node == goal % NODES).astype(jnp.float32)
        curve_row = lax.broadcasted_iota(jnp.int32, (CURVES, 128), 0) == goal // NODES
        points = []
        for d in range(2):
            every = jnp.dot(
                halo_ref[own, d * CURVES : (d + 1) * CURVES, :], hot,
                precision=HIGH, preferred_element_type=jnp.float32,
            )
            points.append(jnp.sum(jnp.where(curve_row, every, 0.0), axis=0, keepdims=True))
        terms = pair_terms(
            points[0], points[1], *(mixed[comp * COLS : (comp + 1) * COLS] for comp in range(4))
        )
        entry = q * 128 + lax.broadcasted_iota(jnp.int32, (1, 128), 1)
        for d in range(2):
            both = terms[d] - 0.5 * terms[2 + d]
            corr = 0.25 * jnp.sum(both[:WIDE], axis=0, keepdims=True) - jnp.sum(
                both[WIDE:], axis=0, keepdims=True
            )
            corr = jnp.where(entry < near_count, corr, 0.0)
            spread = jnp.where(curve_row, corr, 0.0)
            out_ref[me, d] += lax.dot_general(
                spread, hot, NT, precision=HIGH, preferred_element_type=jnp.float32
            )


def make_body(nx, ny):
    cols = halo_cols(ny)
    tiles = (BX + 2) * cols
    smem = pl.BlockSpec(memory_space=pltpu.SMEM)
    vmem = pl.BlockSpec(memory_space=pltpu.VMEM)
    hbm = pl.BlockSpec(memory_space=pltpu.HBM)

    def body(curves, curve_counts, near_counts, near_lists):
        upsample_table, derive_table = spectral_tables(NODES, FINE)
        near = near_lists.shape[-1]
        halo = pl.pallas_call(
            lambda *refs: gather_kernel(nx, ny, *refs),
            name="gather",
            out_shape=jax.ShapeDtypeStruct((BX + 2, cols, PACK, NODES), jnp.float32),
            in_specs=[vmem] * 3,
            out_specs=vmem,
            scratch_shapes=[
                pltpu.SemaphoreType.DMA((4, MEMBERS)),
                pltpu.SemaphoreType.DMA((BX + 2, cols)),
            ],
            compiler_params=pltpu.CompilerParams(collective_id=0, has_side_effects=True),
        )(curves[0, 0], curve_counts, near_counts)
        halo = halo.reshape(tiles, PACK, NODES)
        part = pl.pallas_call(
            lambda *refs: field_kernel(cols, *refs),
            name="near_field",
            out_shape=jax.ShapeDtypeStruct((MEMBERS, 2, CURVES, NODES), jnp.float32),
            in_specs=[smem, vmem] + [hbm] * 4,
            out_specs=vmem,
            scratch_shapes=[
                pltpu.VMEM((tiles, PACK, NODES), jnp.float32),
                pltpu.VMEM((NODES, FINE), jnp.float32),
                pltpu.VMEM((NODES, FINE), jnp.float32),
                pltpu.VMEM((4 * COLS, 128), jnp.float32),
                pltpu.SMEM((tiles, CURVES, NODES), jnp.float32),
                pltpu.VMEM((4, tiles * CURVES, FINE), jnp.float32),
                pltpu.VMEM((tiles * CURVES, 4 * BLOCKS, 8, 128), jnp.float32),
                pltpu.VMEM((9 * CURVES * PANELS, 128), jnp.float32),
                pltpu.VMEM((2, 128, 128), jnp.float32),
                pltpu.VMEM((2, 128, 128), jnp.float32),
                pltpu.VMEM((128, 128), jnp.float32),
                pltpu.SMEM((3, MEMBERS), jnp.int32),
                pltpu.SMEM((10 * CURVES,), jnp.int32),
                pltpu.SMEM((2, 10 * CURVES), jnp.float32),
                pltpu.SMEM((2 * tiles,), jnp.int32),
                pltpu.SemaphoreType.DMA((5,)),
            ],
            compiler_params=pltpu.CompilerParams(vmem_limit_bytes=62 * 1024 * 1024),
        )(
            near_lists[0, 0, 1],
            near_lists[0, 0, 0].reshape(near // 128, 128),
            halo,
            upsample_table,
            derive_table,
            window_table(),
        )
        velocity = pl.pallas_call(
            lambda *refs: return_kernel(nx, ny, *refs),
            name="give_back",
            out_shape=jax.ShapeDtypeStruct((2, CURVES, NODES), jnp.float32),
            in_specs=[vmem] * 2,
            out_specs=vmem,
            scratch_shapes=[
                pltpu.VMEM((MEMBERS, 2, CURVES, NODES), jnp.float32),
                pltpu.SemaphoreType.DMA((MEMBERS,)),
                pltpu.SemaphoreType.DMA((MEMBERS,)),
            ],
            compiler_params=pltpu.CompilerParams(collective_id=1, has_side_effects=True),
        )(part, curve_counts)
        return velocity[None, None]

    return body


def solution(mesh):
    in_specs = (
        P("gx", "gy", None, None, None),
        P("gx", "gy"),
        P("gx", "gy"),
        P("gx", "gy", None, None),
    )
    out_specs = P("gx", "gy", None, None, None)
    body = make_body(mesh.shape["gx"], mesh.shape["gy"])
    return jax.shard_map(body, mesh=mesh, in_specs=in_specs, out_specs=out_specs, check_vma=False)
```

```python
import math

import jax
import jax.numpy as jnp
import numpy as np
from jax import lax
from jax.experimental import pallas as pl
from jax.experimental.pallas import tpu as pltpu
from jax.sharding import PartitionSpec as P

NODES = 128
FINE = 512
PANEL = 16
REFINE = 4
CURVES = 8
PANELS = FINE // PANEL
WIDE = PANEL * REFINE
COLS = WIDE + PANEL
BLOCKS = FINE // 128


SOFT_SQ = 1e-08
HIGH = lax.Precision.HIGHEST
NT = (((1,), (1,)), ((), ()))


def spectral_tables(coarse_count, fine_count):
    coarse_index = np.arange(coarse_count)[:, None, None]
    fine_index = np.arange(fine_count)[None, :, None]
    modes = np.arange(1, coarse_count // 2)[None, None, :]
    nyquist = coarse_count // 2
    offset = 2.0 * np.pi * (fine_index / fine_count - coarse_index / coarse_count)
    upsample_table = (
        1.0 + 2.0 * np.sum(np.cos(modes * offset), axis=-1) + np.cos(nyquist * offset[..., 0])
    ) / coarse_count
    derive_table = (
        -2.0 * np.sum(modes * np.sin(modes * offset), axis=-1)
        - nyquist * np.sin(nyquist * offset[..., 0])
    ) / coarse_count
    return (
        jnp.asarray(upsample_table, dtype=jnp.float32),
        jnp.asarray(derive_table, dtype=jnp.float32),
    )


def lagrange_weights(panel_nodes, refine_factor):
    weights_table = np.zeros((panel_nodes + 3, panel_nodes * refine_factor))
    for column in range(panel_nodes * refine_factor):
        fraction = column % refine_factor / refine_factor
        start_node = column // refine_factor
        weights_table[start_node, column] = -fraction * (fraction - 1.0) * (fraction - 2.0) / 6.0
        weights_table[start_node + 1, column] = (
            (fraction + 1.0) * (fraction - 1.0) * (fraction - 2.0) / 2.0
        )
        weights_table[start_node + 2, column] = (
            -(fraction + 1.0) * fraction * (fraction - 2.0) / 2.0
        )
        weights_table[start_node + 3, column] = (fraction + 1.0) * fraction * (fraction - 1.0) / 6.0
    return np.asarray(weights_table, dtype=np.float32)


def window_table():
    weights = lagrange_weights(PANEL, REFINE)
    table = np.zeros((4 * COLS, 128), dtype=np.float32)
    for comp in range(4):
        for node in range(PANEL + 3):
            table[comp * COLS : comp * COLS + WIDE, comp * 32 + node] = weights[node]
        for node in range(PANEL):
            table[comp * COLS + WIDE + node, comp * 32 + node + 1] = 1.0
    return jnp.asarray(table)


def upsample_all(halo_ref, up_ref, de_ref, fine_ref):
    rows = halo_ref.shape[0] * CURVES
    comps = [
        halo_ref[:, comp * CURVES : (comp + 1) * CURVES, :].reshape(rows, NODES)
        for comp in range(4)
    ]
    up = up_ref[...]
    de = de_ref[...]
    speed = None
    for comp in range(2):
        fine_ref[comp] = jnp.dot(comps[comp], up, precision=HIGH, preferred_element_type=jnp.float32)
        tangent = jnp.dot(comps[comp], de, precision=HIGH, preferred_element_type=jnp.float32)
        speed = tangent * tangent if speed is None else speed + tangent * tangent
    speed = jnp.sqrt(speed) * (2.0 * math.pi / FINE)
    for comp in range(2, 4):
        fine_ref[comp] = speed * jnp.dot(
            comps[comp], up, precision=HIGH, preferred_element_type=jnp.float32
        )


def fine_blocks(fine_ref, tile):
    parts = []
    for comp in range(4):
        value = fine_ref[comp, pl.ds(pl.multiple_of(tile * CURVES, CURVES), CURVES), :]
        parts.append([value[:, 128 * b : 128 * (b + 1)] for b in range(BLOCKS)])
    return parts


def place_sources(tile, fine_ref, src_ref):
    parts = fine_blocks(fine_ref, tile)
    for comp in range(4):
        for b in range(BLOCKS):
            for c in range(CURVES):
                src_ref[tile * CURVES + c, comp * BLOCKS + b] = jnp.broadcast_to(
                    parts[comp][b][c : c + 1], (8, 128)
                )


def place_windows(slot, tile, fine_ref, win_ref):
    lane = lax.broadcasted_iota(jnp.int32, (CURVES, 128), 1)
    shifts = ((slot // 3 - 1).astype(jnp.float32), (slot % 3 - 1).astype(jnp.float32))
    parts = fine_blocks(fine_ref, tile)
    for comp in range(2):
        parts[comp] = [value + shifts[comp] for value in parts[comp]]
    for n in range(PANELS):
        start = (n * PANEL - 1) % FINE
        b, offset = start // 128, start % 128
        row = None
        for comp in range(4):
            shift = (comp * 32 - offset) % 128
            piece = pltpu.roll(parts[comp][b], shift, 1) if shift else parts[comp][b]
            if offset + PANEL + 3 > 128:
                after = parts[comp][(b + 1) % BLOCKS]
                after = pltpu.roll(after, shift, 1) if shift else after
                piece = jnp.where(lane - comp * 32 < 128 - offset, piece, after)
            row = piece if row is None else jnp.where(lane < comp * 32, row, piece)
        win_ref[pl.ds(slot * CURVES * PANELS + n, CURVES, stride=PANELS), :] = row


def pair_terms(tx, ty, px, py, gx, gy):
    rx = tx - px
    ry = ty - py
    dist_sq = rx * rx + ry * ry + SOFT_SQ
    logs = jnp.log(dist_sq)
    proj = (rx * gx + ry * gy) * (1.0 / dist_sq)
    return proj * rx, proj * ry, logs * gx, logs * gy


GROUP = 8


def curve_velocity(pos_x, pos_y, first, last, src_ref, row_ref, move_ref, tgt_ref, acc_ref):
    tgt_ref[0] = jnp.broadcast_to(pos_x, (128, 128)).T
    tgt_ref[1] = jnp.broadcast_to(pos_y, (128, 128)).T

    @pl.loop(0, NODES // (8 * GROUP))
    def block(t):
        base = pl.multiple_of(t * 8 * GROUP, 8 * GROUP)
        txs = [tgt_ref[0, pl.ds(base + 8 * i, 8), :] for i in range(GROUP)]
        tys = [tgt_ref[1, pl.ds(base + 8 * i, 8), :] for i in range(GROUP)]

        def visit(k, accs):
            accs = list(accs)
            row = row_ref[k]
            for b in range(BLOCKS):
                px, py, gx, gy = (src_ref[row, comp * BLOCKS + b] for comp in range(4))
                px = px + move_ref[0, k]
                py = py + move_ref[1, k]
                for i in range(GROUP):
                    terms = pair_terms(txs[i], tys[i], px, py, gx, gy)
                    for j in range(4):
                        accs[4 * i + j] = accs[4 * i + j] + terms[j]
            return tuple(accs)

        zero = jnp.zeros((8, 128), jnp.float32)
        accs = lax.fori_loop(first, last, visit, (zero,) * (4 * GROUP))
        for i in range(GROUP):
            for d in range(2):
                acc_ref[d, pl.ds(base + 8 * i, 8), :] = accs[4 * i + d] - 0.5 * accs[4 * i + 2 + d]

    return [jnp.sum(acc_ref[d].T, axis=0, keepdims=True) for d in range(2)]


BX = 4
BY = 2
MEMBERS = BX * BY
NEAR_COST = 5
PACK = 5 * CURVES
MESH = pl.DeviceIdType.MESH


def halo_cols(size):
    return BY if size == BY else BY + 2


def halo_col(local, cols):
    return local % BY if cols == BY else local + 1


def tile_at(ti, tj, slot, cols):
    return (ti + slot // 3) * cols + halo_col(tj + slot % 3 - 1 + (BY if cols == BY else 0), cols)


def gather_kernel(nx, ny, curves_ref, alive_ref, near_ref, halo_ref, send_sem, recv_sem):
    cols = halo_cols(ny)
    wide = cols > BY
    i, j = lax.axis_index("gx"), lax.axis_index("gy")
    gi, li, gj, lj = i // BX, i % BX, j // BY, j % BY
    own_row, own_col = li + 1, halo_col(lj, cols)
    me = li * BY + lj
    edge = jnp.where((li == 0) | (li == BX - 1), 1, 0)
    to_gi = gi + jnp.where(li == 0, -1, 1)
    to_row = jnp.where(li == 0, BX + 1, 0)
    to_gj = gj + jnp.where(lj == 0, -1, 1)
    to_col = jnp.where(lj == 0, BY + 1, 0)

    def device(x, y):
        return ((x + nx) % nx, (y + ny) % ny)

    def member(bx, by, t):
        return device(bx * BX + t // BY, by * BY + t % BY)

    outer = [(r, c) for r in (0, BX + 1) for c in range(cols)]
    if wide:
        outer += [(r, c) for r in range(1, BX + 1) for c in (0, BY + 1)]

    barrier = pltpu.get_barrier_semaphore()
    for t in range(1, MEMBERS):
        pl.semaphore_signal(
            barrier, inc=1, device_id=member(gi, gj, (me + t) % MEMBERS), device_id_type=MESH
        )
    for r, c in outer:
        pl.semaphore_signal(
            barrier,
            inc=1,
            device_id=device(gi * BX + r - 1, gj * BY + c - (1 if wide else 0)),
            device_id_type=MESH,
        )

    living = lax.broadcasted_iota(jnp.int32, (CURVES, NODES), 0) < alive_ref[...]
    for comp in range(4):
        value = curves_ref[comp]
        halo_ref[own_row, own_col, comp * CURVES : (comp + 1) * CURVES, :] = (
            value if comp < 2 else jnp.where(living, value, 0.0)
        )
    numbers = jnp.where(
        lax.broadcasted_iota(jnp.int32, (CURVES, NODES), 0) == 0, alive_ref[...], near_ref[...]
    )
    halo_ref[own_row, own_col, 4 * CURVES :, :] = numbers.astype(jnp.float32)

    scale = 2 if wide else 1
    pl.semaphore_wait(barrier, MEMBERS * scale - 1 + edge * (MEMBERS * scale))

    def copy(kind, t, row, col, target):
        return pltpu.make_async_remote_copy(
            src_ref=halo_ref.at[own_row, own_col],
            dst_ref=halo_ref.at[row, col],
            send_sem=send_sem.at[kind, t],
            recv_sem=recv_sem.at[row, col],
            device_id=target,
            device_id_type=MESH,
        )

    always = [
        copy(0, t, own_row, own_col, member(gi, gj, (me + t) % MEMBERS))
        for t in range(1, MEMBERS)
    ]
    edges = [copy(1, t, to_row, own_col, member(to_gi, gj, t)) for t in range(MEMBERS)]
    if wide:
        always += [copy(2, t, own_row, to_col, member(gi, to_gj, t)) for t in range(MEMBERS)]
        edges += [copy(3, t, to_row, to_col, member(to_gi, to_gj, t)) for t in range(MEMBERS)]

    @pl.when(edge == 1)
    def _():
        for item in edges:
            item.start()

    for item in always:
        item.start()

    other = member(gi, gj, (me + 1) % MEMBERS)
    for t in range(1, MEMBERS):
        source = (me + t) % MEMBERS
        copy(0, t, source // BY + 1, halo_col(source % BY, cols), other).wait_recv()
    for r, c in outer:
        copy(0, 1, r, c, other).wait_recv()
    for item in always:
        item.wait_send()

    @pl.when(edge == 1)
    def _():
        for item in edges:
            item.wait_send()


def return_kernel(nx, ny, part_ref, alive_ref, out_ref, got_ref, send_sem, recv_sem):
    i, j = lax.axis_index("gx"), lax.axis_index("gy")
    gi, gj = i // BX, j // BY
    me = i % BX * BY + j % BY

    def member(t):
        return (gi * BX + t // BY, gj * BY + t % BY)

    barrier = pltpu.get_barrier_semaphore()
    for t in range(1, MEMBERS):
        pl.semaphore_signal(
            barrier, inc=1, device_id=member((me + t) % MEMBERS), device_id_type=MESH
        )
    pl.semaphore_wait(barrier, MEMBERS - 1)
    copies = []
    for t in range(1, MEMBERS):
        target = (me + t) % MEMBERS
        copies.append(
            pltpu.make_async_remote_copy(
                src_ref=part_ref.at[target],
                dst_ref=got_ref.at[t],
                send_sem=send_sem.at[t],
                recv_sem=recv_sem.at[t],
                device_id=member(target),
                device_id_type=MESH,
            )
        )
        copies[-1].start()
    total = part_ref[me]
    for t in range(1, MEMBERS):
        copies[t - 1].wait_recv()
        total = total + got_ref[t]
    alive = lax.broadcasted_iota(jnp.int32, (CURVES, NODES), 0) < alive_ref[...]
    for d in range(2):
        out_ref[d] = jnp.where(alive, total[d], 0.0)
    for item in copies:
        item.wait_send()


def field_kernel(
    cols, panel_ref, goal_ref, halo_hbm, up_hbm, de_hbm, mix_hbm, out_ref,
    halo_ref, up_ref, de_ref, mix_ref, number_ref,
    fine_ref, src_ref, win_ref, tgt_ref, acc_ref, near_ref, work_ref, row_ref, move_ref, count_ref, sem,
):
    tiles = (BX + 2) * cols
    loads = [
        pltpu.make_async_copy(source, target, sem.at[n])
        for n, (source, target) in enumerate(
            (
                (halo_hbm, halo_ref),
                (up_hbm, up_ref),
                (de_hbm, de_ref),
                (mix_hbm, mix_ref),
                (halo_hbm.at[:, pl.ds(4 * CURVES, CURVES), :], number_ref),
            )
        )
    ]
    for item in loads:
        item.start()
    for item in loads:
        item.wait()

    @pl.loop(0, tiles)
    def numbers(tile):
        for n in range(2):
            count_ref[2 * tile + n] = number_ref[tile, n, 0].astype(jnp.int32)

    li, lj = lax.axis_index("gx") % BX, lax.axis_index("gy") % BY
    me = li * BY + lj
    upsample_all(halo_ref, up_ref, de_ref, fine_ref)
    out_ref[...] = jnp.zeros_like(out_ref)

    @pl.loop(0, (BX + 2) * cols)
    def place(tile):
        place_sources(tile, fine_ref, src_ref)

    @pl.loop(0, 9)
    def windows(slot):
        place_windows(slot, tile_at(li, lj, slot, cols), fine_ref, win_ref)

    def survey(t, carry):
        pairs, near = carry
        own = tile_at(t // BY, t % BY, 4, cols)
        sources = 0
        for slot in range(9):
            sources = sources + count_ref[2 * tile_at(t // BY, t % BY, slot, cols)]
        cost = (count_ref[2 * own + 1] + 127) // 128 * NEAR_COST
        work_ref[0, t] = sources
        work_ref[1, t] = pairs
        work_ref[2, t] = cost
        return pairs + sources * count_ref[2 * own], near + cost

    pairs, near = lax.fori_loop(0, MEMBERS, survey, (0, 0))
    quota = (pairs + near + MEMBERS - 1) // MEMBERS
    low = lax.fori_loop(
        0, me, lambda t, total: total + jnp.maximum(quota - work_ref[2, t], 0), 0
    )
    high = jnp.minimum(low + jnp.maximum(quota - work_ref[2, me], 0), pairs)
    low = jnp.minimum(low, pairs)

    @pl.loop(0, MEMBERS)
    def member(t):
        ti, tj = t // BY, t % BY
        own = tile_at(ti, tj, 4, cols)
        sources, base, curves = work_ref[0, t], work_ref[1, t], count_ref[2 * own]

        @pl.when((low < base + sources * curves) & (high > base))
        def _():
            def enlist(slot, first):
                tile = tile_at(ti, tj, slot, cols)
                for c in range(CURVES):
                    row_ref[first + c] = tile * CURVES + c
                    move_ref[0, first + c] = (slot // 3 - 1).astype(jnp.float32)
                    move_ref[1, first + c] = (slot % 3 - 1).astype(jnp.float32)
                return first + count_ref[2 * tile]

            lax.fori_loop(0, 9, enlist, 0)

            @pl.loop(0, curves)
            def curve(c):
                first = jnp.clip(low - base - c * sources, 0, sources)
                last = jnp.clip(high - base - c * sources, 0, sources)

                @pl.when(first < last)
                def _():
                    vel = curve_velocity(
                        halo_ref[own, pl.ds(c, 1), :], halo_ref[own, pl.ds(CURVES + c, 1), :],
                        first, last, src_ref, row_ref, move_ref, tgt_ref, acc_ref,
                    )
                    for d in range(2):
                        out_ref[t, d, pl.ds(c, 1), :] = vel[d]

    own = tile_at(li, lj, 4, cols)
    near_count = count_ref[2 * own + 1]

    @pl.loop(0, (near_count + 127) // 128)
    def chunk(q):
        @pl.loop(0, 16)
        def fetch(h):
            for j in range(8):
                near_ref[pl.ds(h * 8 + j, 1), :] = win_ref[pl.ds(panel_ref[1, q * 128 + h * 8 + j], 1), :]

        mixed = lax.dot_general(
            mix_ref[...], near_ref[...], NT, precision=HIGH, preferred_element_type=jnp.float32
        )
        goal = goal_ref[0:1, pl.ds(pl.multiple_of(q * 128, 128), 128)]
        node = lax.broadcasted_iota(jnp.int32, (128, 128), 0)
        hot = (node == goal % NODES).astype(jnp.float32)
        curve_row = lax.broadcasted_iota(jnp.int32, (CURVES, 128), 0) == goal // NODES
        points = []
        for d in range(2):
            every = jnp.dot(
                halo_ref[own, d * CURVES : (d + 1) * CURVES, :], hot,
                precision=HIGH, preferred_element_type=jnp.float32,
            )
            points.append(jnp.sum(jnp.where(curve_row, every, 0.0), axis=0, keepdims=True))
        terms = pair_terms(
            points[0], points[1], *(mixed[comp * COLS : (comp + 1) * COLS] for comp in range(4))
        )
        entry = q * 128 + lax.broadcasted_iota(jnp.int32, (1, 128), 1)
        for d in range(2):
            both = terms[d] - 0.5 * terms[2 + d]
            corr = 0.25 * jnp.sum(both[:WIDE], axis=0, keepdims=True) - jnp.sum(
                both[WIDE:], axis=0, keepdims=True
            )
            corr = jnp.where(entry < near_count, corr, 0.0)
            spread = jnp.where(curve_row, corr, 0.0)
            out_ref[me, d] += lax.dot_general(
                spread, hot, NT, precision=HIGH, preferred_element_type=jnp.float32
            )


def make_body(nx, ny):
    cols = halo_cols(ny)
    tiles = (BX + 2) * cols
    smem = pl.BlockSpec(memory_space=pltpu.SMEM)
    vmem = pl.BlockSpec(memory_space=pltpu.VMEM)
    hbm = pl.BlockSpec(memory_space=pltpu.HBM)

    def body(curves, curve_counts, near_counts, near_lists):
        upsample_table, derive_table = spectral_tables(NODES, FINE)
        halo = pl.pallas_call(
            lambda *refs: gather_kernel(nx, ny, *refs),
            name="gather",
            out_shape=jax.ShapeDtypeStruct((BX + 2, cols, PACK, NODES), jnp.float32),
            in_specs=[vmem] * 3,
            out_specs=vmem,
            scratch_shapes=[
                pltpu.SemaphoreType.DMA((4, MEMBERS)),
                pltpu.SemaphoreType.DMA((BX + 2, cols)),
            ],
            compiler_params=pltpu.CompilerParams(collective_id=0, has_side_effects=True),
        )(curves[0, 0], curve_counts, near_counts)
        halo = halo.reshape(tiles, PACK, NODES)
        part = pl.pallas_call(
            lambda *refs: field_kernel(cols, *refs),
            name="near_field",
            out_shape=jax.ShapeDtypeStruct((MEMBERS, 2, CURVES, NODES), jnp.float32),
            in_specs=[smem, vmem] + [hbm] * 4,
            out_specs=vmem,
            scratch_shapes=[
                pltpu.VMEM((tiles, PACK, NODES), jnp.float32),
                pltpu.VMEM((NODES, FINE), jnp.float32),
                pltpu.VMEM((NODES, FINE), jnp.float32),
                pltpu.VMEM((4 * COLS, 128), jnp.float32),
                pltpu.SMEM((tiles, CURVES, NODES), jnp.float32),
                pltpu.VMEM((4, tiles * CURVES, FINE), jnp.float32),
                pltpu.VMEM((tiles * CURVES, 4 * BLOCKS, 8, 128), jnp.float32),
                pltpu.VMEM((9 * CURVES * PANELS, 128), jnp.float32),
                pltpu.VMEM((2, 128, 128), jnp.float32),
                pltpu.VMEM((2, 128, 128), jnp.float32),
                pltpu.VMEM((128, 128), jnp.float32),
                pltpu.SMEM((3, MEMBERS), jnp.int32),
                pltpu.SMEM((10 * CURVES,), jnp.int32),
                pltpu.SMEM((2, 10 * CURVES), jnp.float32),
                pltpu.SMEM((2 * tiles,), jnp.int32),
                pltpu.SemaphoreType.DMA((5,)),
            ],
            compiler_params=pltpu.CompilerParams(vmem_limit_bytes=62 * 1024 * 1024),
        )(
            near_lists[0, 0],
            near_lists[0, 0],
            halo,
            upsample_table,
            derive_table,
            window_table(),
        )
        velocity = pl.pallas_call(
            lambda *refs: return_kernel(nx, ny, *refs),
            name="give_back",
            out_shape=jax.ShapeDtypeStruct((2, CURVES, NODES), jnp.float32),
            in_specs=[vmem] * 2,
            out_specs=vmem,
            scratch_shapes=[
                pltpu.VMEM((MEMBERS, 2, CURVES, NODES), jnp.float32),
                pltpu.SemaphoreType.DMA((MEMBERS,)),
                pltpu.SemaphoreType.DMA((MEMBERS,)),
            ],
            compiler_params=pltpu.CompilerParams(collective_id=1, has_side_effects=True),
        )(part, curve_counts)
        return velocity[None, None]

    return body


def solution(mesh):
    in_specs = (
        P("gx", "gy", None, None, None),
        P("gx", "gy"),
        P("gx", "gy"),
        P("gx", "gy", None, None),
    )
    out_specs = P("gx", "gy", None, None, None)
    body = make_body(mesh.shape["gx"], mesh.shape["gy"])
    return jax.shard_map(body, mesh=mesh, in_specs=in_specs, out_specs=out_specs, check_vma=False)
```
